32 devices in a mesh: gx: 4 (over z), gy: 4 (over y, core), gz: 2 (over x).
Axes of the slice: x: 2, y: 2, z: 4, core: 2. Of those that a mesh axis runs over, the one named last changes fastest.
Arguments:
- offsets: float32 [3, 8, 8, 2, 128], P(None, 'gx', 'gy', 'gz'), may hold values from 0 to 1
- velocity: float32 [3, 8, 8, 2, 128], P(None, 'gx', 'gy', 'gz'), may hold values from -6 to 6
- density: float32 [8, 8, 2, 128], P('gx', 'gy', 'gz'), may hold values from 0.92 to 1.08
- counts: int32 [8, 8, 2], P('gx', 'gy', 'gz'), may hold values from 64 to 128, as said below
Outputs:
- offsets_out: float32 [3, 8, 8, 2, 128], P(None, 'gx', 'gy', 'gz')
- velocity_out: float32 [3, 8, 8, 2, 128], P(None, 'gx', 'gy', 'gz')
- density_out: float32 [8, 8, 2, 128], P('gx', 'gy', 'gz')
The draws below stay inside these ranges and needn't reach their ends.
Inputs may be any that keep to these rules, and one draw needn't show every extreme that they name: `counts`: A bin's particles fill its slots 0 to count - 1; some bin is full.
All inputs are finite; a program needn't handle non-finite values.
Results may differ from the reference program's by a relative error of at most 0.0003.
Values sent between devices are 32-bit elements; how exact they have to be, the bound alone decides.
No kernel may reach another device: no remote copies, remote signals or barrier semaphores. Data moves between devices by JAX's collectives and lax.ppermute only.
A program may use at most 64 MiB of HBM per device.

```python
import math
import jax
import jax.numpy as jnp
from jax import lax

P_SIZE = 128
NBX = 8
NBY = 8
NBZ = 2


def draw_counts(key, part):
    raw = jax.random.randint(key, (NBX, NBY, NBZ), 1, P_SIZE + 1)
    layers = jnp.arange(NBZ, dtype=jnp.int32)
    distance = jnp.abs(2 * layers - (NBZ - 1))
    weight = 4 - jnp.minimum(distance * 4 // NBZ, 3)
    filled = P_SIZE // 2 + (raw - 1) * weight[None, None, :] // 8
    filled = filled.at[0, 0, NBZ // 2].set(P_SIZE)
    filled = filled.at[NBX - 1, NBY - 1, 0].set(P_SIZE // 2)
    return filled.astype(jnp.int32)


def steps_of(own_key, shape, shards, least, high):
    level = 1.0
    for position, shards_of in shards:
        heights = jax.random.uniform(jax.random.fold_in(jax.random.fold_in(own_key, 6), position), (shards_of,), jnp.float32, least / len(shards), high / len(shards))
        level = level * jnp.repeat(jnp.exp(heights), shape[position] // shards_of).reshape((-1,) + (1,) * (len(shape) - 1 - position))
    return level


def gaussian(own_key, extent, spread, reach, cuts=(), held_as=jnp.bfloat16):
    drawn = jax.random.normal(own_key, extent, jnp.float32) * spread
    if len(cuts) > 0:
        drawn = steps_of(own_key, extent, cuts, -0.22, 0.18) * drawn
    return jnp.clip(drawn, min=-reach, max=reach).astype(held_as)


def setup_inputs(seed: int = 0) -> dict:
    key_list = jax.random.split(jax.random.key(seed), 5)
    offsets = jnp.clip(1.0 * jax.random.uniform(key_list[0], (3, NBX, NBY, NBZ, P_SIZE), jnp.float32) ** steps_of(key_list[0], (3, NBX, NBY, NBZ, P_SIZE), ((1, 4), (2, 4), (3, 2)), -0.2, 0.2), 0.0, 1.0)
    velocity = gaussian(key_list[1], (3, NBX, NBY, NBZ, P_SIZE), 1.0, 6.0, ((1, 4), (2, 4), (3, 2)), jnp.float32)
    density = jnp.clip(0.92 + 0.16000003 * jax.random.uniform(key_list[2], (NBX, NBY, NBZ, P_SIZE), jnp.float32) ** steps_of(key_list[2], (NBX, NBY, NBZ, P_SIZE), ((0, 4), (1, 4), (2, 2)), -0.2, 0.2), 0.92, 1.08)
    counts = draw_counts(jax.random.fold_in(key_list[4], 71), 0)
    return dict(offsets=offsets, velocity=velocity, density=density, counts=counts)


H_SMOOTH = 0.5
KERNEL_NORM = 21.0 / (16.0 * math.pi * H_SMOOTH ** 3)
SOUND_SPEED = 10.0
STIFFNESS = SOUND_SPEED * SOUND_SPEED / 7.0
VISC_ALPHA = 0.1
TIME_STEP = 0.01
GRAVITY = -2.0

def advance(padded):
    width_x = padded.shape[1] - 2
    width_y = padded.shape[2] - 2
    width_z = padded.shape[3] - 2
    slots = padded.shape[4]
    nbins = width_x * width_y * width_z
    dens_all = padded[6]
    ratio_all = STIFFNESS * (dens_all ** 7 - 1.0) / (dens_all * dens_all)
    extended = jnp.concatenate([padded, ratio_all[None]], axis=0)
    inner = extended[:, 1:-1, 1:-1, 1:-1].reshape(9, nbins, slots)
    particle_mass = 2.0 / slots
    grad_scale = particle_mass * (-5.0 * KERNEL_NORM / (H_SMOOTH * H_SMOOTH))
    zero_index = jnp.zeros((), jnp.int32)

    def visit(counter, totals):
        counter = counter.astype(jnp.int32)
        shift_x = counter // 9
        shift_y = counter // 3 % 3
        shift_z = counter % 3
        nearby = lax.dynamic_slice(extended, (zero_index, shift_x, shift_y, shift_z, zero_index), (9, width_x, width_y, width_z, slots)).reshape(9, nbins, slots)
        shifts = (shift_x, shift_y, shift_z)
        separation = [inner[c][:, :, None] - nearby[c][:, None, :] + (shifts[c] - 1).astype(jnp.float32) for c in range(3)]
        dist_sq = separation[0] * separation[0] + separation[1] * separation[1] + separation[2] * separation[2]
        radius = jnp.sqrt(dist_sq) / H_SMOOTH
        base = jnp.maximum(1.0 - 0.5 * radius, 0.0)
        weight = nearby[7][:, None, :] * grad_scale * base * base * base
        approach = sum(((inner[3 + c][:, :, None] - nearby[3 + c][:, None, :]) * separation[c] for c in range(3)))
        mean_density = 0.5 * (inner[6][:, :, None] + nearby[6][:, None, :])
        closing = H_SMOOTH * jnp.minimum(approach, 0.0) / (dist_sq + 0.01 * H_SMOOTH * H_SMOOTH)
        coupling = inner[8][:, :, None] + nearby[8][:, None, :] - VISC_ALPHA * SOUND_SPEED * closing / mean_density
        force = weight * coupling
        parts = [-lax.optimization_barrier(jnp.sum(force * separation[c], axis=-1)) for c in range(3)]
        parts.append(lax.optimization_barrier(jnp.sum(weight * approach, axis=-1)))
        return totals + jnp.stack(parts, axis=0)
    totals = lax.fori_loop(0, 27, visit, jnp.zeros((4, nbins, slots), jnp.float32))
    gravity = jnp.array([0.0, 0.0, GRAVITY], jnp.float32)[:, None, None]
    velocity_new = inner[3:6] + TIME_STEP * (totals[0:3] + gravity)
    density_new = inner[6] + TIME_STEP * totals[3]
    offsets_new = inner[0:3] + TIME_STEP * velocity_new
    updated = jnp.concatenate([offsets_new, velocity_new, density_new[None]], axis=0)
    kept = jnp.where(inner[7][None] > 0.5, updated, inner[0:7])
    result = jnp.concatenate([kept, inner[7:8]], axis=0)
    return result.reshape(8, width_x, width_y, width_z, slots)

def reference(offsets, velocity, density, counts):
    slot_ids = jnp.arange(P_SIZE, dtype=jnp.int32)
    live = (slot_ids[None, None, None, :] < counts[..., None]).astype(jnp.float32)
    state = jnp.concatenate([offsets, velocity, density[None], live[None]], axis=0)
    zero_index = jnp.zeros((), jnp.int32)
    for repeat in range(2):
        padded = jnp.pad(state, ((0, 0), (1, 1), (1, 1), (1, 1), (0, 0)), mode='wrap')

        def column(start):
            slab = lax.dynamic_slice(padded, (zero_index, start.astype(jnp.int32), zero_index, zero_index, zero_index), (8, 3, NBY + 2, NBZ + 2, P_SIZE))
            return advance(slab)[:, 0]
        state = jnp.moveaxis(lax.map(column, jnp.arange(NBX, dtype=jnp.int32)), 0, 1)
    state = jnp.roll(state, -1, axis=1)
    mask = state[7]
    return (state[0:3] * mask[None], state[3:6] * mask[None], state[6] * mask)
```

```python
import functools
import math

import jax
import jax.numpy as jnp
from jax import lax
from jax.experimental import pallas as pl
from jax.experimental.pallas import tpu as pltpu
from jax.sharding import PartitionSpec as P

H_SMOOTH = 0.5
KERNEL_NORM = 21.0 / (16.0 * math.pi * H_SMOOTH**3)
SOUND_SPEED = 10.0
STIFFNESS = SOUND_SPEED * SOUND_SPEED / 7.0
VISC_ALPHA = 0.1
TIME_STEP = 0.01
GRAVITY = -2.0
FAR = 1000.0
LIVE_BELOW = 500.0
ROWS = 8
CHUNK = 16


def ratio_of(rho):
    square = rho * rho
    return STIFFNESS * (square * square * square * rho - 1.0) / square


def pack(offsets, velocity, density, counts):
    slots = offsets.shape[-1]
    ids = jnp.arange(slots, dtype=jnp.int32)
    live = ids < counts[..., None]
    rows = [
        jnp.where(live, offsets[0], FAR),
        offsets[1],
        offsets[2],
        velocity[0],
        velocity[1],
        velocity[2],
        density,
        ratio_of(density),
    ]
    return jnp.stack(rows, axis=-2)


def neighbours(first, last, axis):
    size = lax.axis_size(axis)
    even = lax.axis_index(axis) % 2 == 0
    ones = [(i, i ^ 1) for i in range(size)]
    twos = [(i, ((i + 1) ^ 1) - 1) for i in range(size)]
    twos = [(i, j % size) for i, j in twos]
    got_two = lax.ppermute(jnp.where(even, first, last), axis, twos)
    got_one = lax.ppermute(jnp.where(even, last, first), axis, ones)
    before = jnp.where(even, got_two, got_one)
    after = jnp.where(even, got_one, got_two)
    return before, after


def from_after(value, axis, steps=1):
    size = lax.axis_size(axis)
    return lax.ppermute(value, axis, [((i + steps) % size, i) for i in range(size)])


def pair_kernel(tgt_ref, src_ref, *rest, targets, cells, slots, final):
    if final:
        off_ref, vel_ref, den_ref, cell_ref, col_ref, sum_ref = rest
    else:
        out_ref, cell_ref, col_ref, sum_ref = rest
    row = lax.broadcasted_iota(jnp.int32, (ROWS, slots), 0)

    def placed(tile, position):
        shift = jnp.where(row == 0, float(position[0]), 0.0)
        shift = jnp.where(row == 1, float(position[1]), shift)
        shift = jnp.where(row == 2, float(position[2]), shift)
        return tile - shift

    for k, (index, position) in enumerate(cells):
        cell_ref[k] = placed(src_ref[index], position)

    particle_mass = 2.0 / slots
    scale = particle_mass * (-5.0 * KERNEL_NORM / (H_SMOOTH * H_SMOOTH))
    visc = 2.0 * VISC_ALPHA * SOUND_SPEED * H_SMOOTH
    eps = 0.01 * H_SMOOTH * H_SMOOTH
    lane = lax.broadcasted_iota(jnp.int32, (slots, slots), 1)

    for index, position, triples in targets:
        tile = tgt_ref[index]
        cols = placed(tile, position).T
        for c in range(ROWS):
            col_ref[c] = jnp.broadcast_to(cols[:, c : c + 1], (slots, slots))
        live_count = jnp.sum((tile[0:1] < LIVE_BELOW).astype(jnp.int32))
        chunks = (live_count + CHUNK - 1) // CHUNK

        def chunk_body(step, carry):
            at = pl.ds(pl.multiple_of(step * CHUNK, CHUNK), CHUNK)
            xi, yi, zi, ui, vi, wi, rhoi, ratioi = [col_ref[c, at, :] for c in range(ROWS)]

            def visit(cell, sums):
                xj, yj, zj, uj, vj, wj, rhoj, ratioj = [
                    cell_ref[cell, c : c + 1, :] for c in range(ROWS)
                ]
                dx = xi - xj
                dy = yi - yj
                dz = zi - zj
                dist = dx * dx + dy * dy + dz * dz
                approach = (ui - uj) * dx + (vi - vj) * dy + (wi - wj) * dz
                safe = jnp.maximum(dist, 1e-30)
                radius = safe * lax.rsqrt(safe)
                base = jnp.maximum(1.0 - radius * (0.5 / H_SMOOTH), 0.0)
                weight = base * base * base
                below = (dist + eps) * (rhoi + rhoj)
                closing = (visc * jnp.minimum(approach, 0.0)) / below
                force = weight * ((ratioi + ratioj) - closing)
                return (
                    sums[0] + force * dx,
                    sums[1] + force * dy,
                    sums[2] + force * dz,
                    sums[3] + weight * approach,
                )

            def group(g, sums):
                start = triples[0] + (g // 3) * triples[1] + (g % 3) * triples[2]
                for d in range(3):
                    sums = visit(start + d, sums)
                return sums

            zero = jnp.zeros((CHUNK, slots), jnp.float32)
            sums = lax.fori_loop(0, 9, group, (zero, zero, zero, zero))
            for c in range(4):
                sum_ref[c, at, :] = sums[c]
            return carry

        lax.fori_loop(0, chunks, chunk_body, 0)
        joined = None
        for c in range(4):
            total = jnp.sum(sum_ref[c], axis=-1, keepdims=True)
            joined = total if joined is None else jnp.where(lane == c, total, joined)
        totals = jnp.broadcast_to(joined, (slots, slots)).T
        live = tile[0:1] < LIVE_BELOW
        new_vel = [
            tile[3 + c : 4 + c]
            + TIME_STEP * (-scale * totals[c : c + 1] + (GRAVITY if c == 2 else 0.0))
            for c in range(3)
        ]
        new_rho = tile[6:7] + TIME_STEP * scale * totals[3:4]
        new_off = [tile[c : c + 1] + TIME_STEP * new_vel[c] for c in range(3)]
        if final:
            tx, ty, tz = index_out(position)
            for c in range(3):
                off_ref[c, tx, ty, tz, :] = jnp.where(live, new_off[c], 0.0)[0]
                vel_ref[c, tx, ty, tz, :] = jnp.where(live, new_vel[c], 0.0)[0]
            den_ref[tx, ty, tz, :] = jnp.where(live, new_rho, 0.0)[0]
        else:
            updated = jnp.concatenate(new_off + new_vel + [new_rho, ratio_of(new_rho)], axis=0)
            out_ref[index_out(position)] = jnp.where(live, updated, tile)


def index_out(position):
    return position


def advance(src, first_target, shape, z_index, z_out, final):
    nx, ny = shape
    slots = src.shape[-1]
    z_low = z_out[0] - 1
    zs = len(z_out) + 2
    cells = []
    for cx in range(nx + 2):
        for cy in range(ny + 2):
            for cz in range(zs):
                z = z_low + cz
                cells.append(((cx, cy, z_index(z)), (cx - 1, cy - 1, z)))
    targets = []
    for tx in range(nx):
        for ty in range(ny):
            for tz in z_out:
                start = (tx * (ny + 2) + ty) * zs + (tz - z_out[0])
                targets.append(
                    (
                        (tx + 1, ty + 1, z_index(tz)),
                        (tx, ty, tz),
                        (start, (ny + 2) * zs, zs),
                    )
                )
    if final:
        out_shape = (
            jax.ShapeDtypeStruct((3, nx, ny, len(z_out), slots), jnp.float32),
            jax.ShapeDtypeStruct((3, nx, ny, len(z_out), slots), jnp.float32),
            jax.ShapeDtypeStruct((nx, ny, len(z_out), slots), jnp.float32),
        )
    else:
        out_shape = jax.ShapeDtypeStruct((nx, ny, len(z_out), ROWS, slots), jnp.float32)
    base = z_out[0]
    targets = [(i, p[:2] + (p[2],), t) for i, p, t in targets]

    def kernel(src_ref, *rest):
        pair_kernel(src_ref, src_ref, *rest, targets=targets, cells=cells, slots=slots, final=final)

    assert base == 0
    vmem = pl.BlockSpec(memory_space=pltpu.VMEM)
    return pl.pallas_call(
        kernel,
        out_shape=out_shape,
        in_specs=[vmem],
        out_specs=jax.tree.map(lambda _: vmem, out_shape),
        scratch_shapes=[
            pltpu.VMEM((len(cells), ROWS, slots), jnp.float32),
            pltpu.VMEM((ROWS, slots, slots), jnp.float32),
            pltpu.VMEM((4, slots, slots), jnp.float32),
        ],
    )(src)


def per_device(offsets, velocity, density, counts):
    wide, tall, deep = offsets.shape[1:4]
    tile = pack(offsets, velocity, density, counts)
    stacks = lax.axis_size("gz")
    layers = stacks * deep
    parts = [tile] + [from_after(tile, "gz", k) for k in range(1, stacks)]
    column = jnp.concatenate(parts, axis=2)

    def widen(block, axis, dim):
        before, after = neighbours(
            lax.slice_in_dim(block, 0, 1, axis=dim),
            lax.slice_in_dim(block, block.shape[dim] - 1, block.shape[dim], axis=dim),
            axis,
        )
        return jnp.concatenate([before, block, after], axis=dim)

    first_in = widen(widen(column, "gy", 1), "gx", 0)
    if layers <= deep + 2:
        targets = list(range(layers))
        shift = 0
    else:
        targets = list(range(deep + 2))
        shift = -1
    first = advance(first_in, 0, (wide, tall), lambda z: (z + shift) % layers, targets, False)
    second_in = widen(first, "gy", 1)
    second_in = jnp.concatenate([second_in, from_after(second_in[0:2], "gx")], axis=0)
    held = len(targets)
    return advance(
        second_in, 0, (wide, tall), lambda z: (z - shift) % held, list(range(deep)), True
    )


def solution(mesh):
    return jax.shard_map(
        per_device,
        mesh=mesh,
        in_specs=(
            P(None, "gx", "gy", "gz", None),
            P(None, "gx", "gy", "gz", None),
            P("gx", "gy", "gz", None),
            P("gx", "gy", "gz"),
        ),
        out_specs=(
            P(None, "gx", "gy", "gz", None),
            P(None, "gx", "gy", "gz", None),
            P("gx", "gy", "gz", None),
        ),
        check_vma=False,
    )
```

```python
import functools
import math

import jax
import jax.numpy as jnp
from jax import lax
from jax.experimental import pallas as pl
from jax.experimental.pallas import tpu as pltpu
from jax.sharding import PartitionSpec as P

H_SMOOTH = 0.5
KERNEL_NORM = 21.0 / (16.0 * math.pi * H_SMOOTH**3)
SOUND_SPEED = 10.0
STIFFNESS = SOUND_SPEED * SOUND_SPEED / 7.0
VISC_ALPHA = 0.1
TIME_STEP = 0.01
GRAVITY = -2.0
FAR = 1000.0
LIVE_BELOW = 500.0
ROWS = 8
UNROLL = 3
FORMS = 3
ITEMS = 6


def ratio_of(rho):
    square = rho * rho
    return STIFFNESS * (square * square * square * rho - 1.0) / square


def pack(offsets, velocity, density, counts):
    slots = offsets.shape[-1]
    ids = jnp.arange(slots, dtype=jnp.int32)
    live = ids < counts[..., None]
    rows = [
        jnp.where(live, offsets[0], FAR),
        offsets[1],
        offsets[2],
        velocity[0],
        velocity[1],
        velocity[2],
        density,
        ratio_of(density),
    ]
    return jnp.stack(rows, axis=-2)


def neighbours(first, last, axis):
    size = lax.axis_size(axis)
    even = lax.axis_index(axis) % 2 == 0
    ones = [(i, i ^ 1) for i in range(size)]
    twos = [(i, ((i + 1) ^ 1) - 1) for i in range(size)]
    twos = [(i, j % size) for i, j in twos]
    got_two = lax.ppermute(jnp.where(even, first, last), axis, twos)
    got_one = lax.ppermute(jnp.where(even, last, first), axis, ones)
    before = jnp.where(even, got_two, got_one)
    after = jnp.where(even, got_one, got_two)
    return before, after


def from_after(value, axis, steps=1):
    size = lax.axis_size(axis)
    return lax.ppermute(value, axis, [((i + steps) % size, i) for i in range(size)])


def split3(value):
    high = value.astype(jnp.bfloat16)
    rest = value - high.astype(jnp.float32)
    middle = rest.astype(jnp.bfloat16)
    low = (rest - middle.astype(jnp.float32)).astype(jnp.bfloat16)
    return high, middle, low


LEFT_TERMS = (0, 0, 0, 1, 1, 2, 1, 2)
RIGHT_TERMS = (0, 1, 2, 0, 1, 0, 2, 1)


def pair_kernel(*refs, targets, columns, ranges, slots, layers_of, has_part, final):
    own_ref, src_ref = refs[:2]
    part_ref = refs[2] if has_part else None
    outs = refs[2 + has_part : -11]
    pack_ref, feat_ref, point_ref, left_ref, acc_ref, sum_ref = refs[-11:-5]
    even_ref, odd_ref, ratio_ref, count_ref, item_ref = refs[-5:]
    nx, ny, nz = targets
    tall, deep = src_ref.shape[1:3]
    ncol = len(columns)
    row = lax.broadcasted_iota(jnp.int32, (ROWS, slots), 0)
    lane = lax.broadcasted_iota(jnp.int32, (ROWS, slots), 1)
    far_tile = jnp.where(row == 0, FAR, 0.0)
    first3 = row < 3
    eps = 0.01 * H_SMOOTH * H_SMOOTH
    visc = 2.0 * VISC_ALPHA * SOUND_SPEED * H_SMOOTH
    particle_mass = 2.0 / slots
    scale = particle_mass * (-5.0 * KERNEL_NORM / (H_SMOOTH * H_SMOOTH))
    middle = 1.0 - 0.5 * nx
    slot_bits = slots.bit_length() - 1
    assert slots == 1 << slot_bits
    short = (3 * slots) // 4
    idle = feat_ref.shape[0] // UNROLL - 1

    def live_in(tile_row):
        return jnp.sum(jnp.where(tile_row < LIVE_BELOW, 1, 0))

    for a in range(ncol):
        for b in range(tall):
            for c in range(deep):
                count_ref[(a * tall + b) * deep + c] = live_in(src_ref[a, b, c, 0:1])

    def by_row(default, **kinds):
        result = default
        for name, value in kinds.items():
            result = jnp.where(row == int(name[1:]), value, result)
        return result

    def common(rows):
        x, y, z, u, v, w, rho, _ = rows
        square = x * x + y * y + z * z
        inner = u * x + v * y + w * z
        return square, inner, rho * (square + eps)

    def features(k):
        tile = pack_ref[k]
        rows = [pack_ref[k, c : c + 1, :] for c in range(ROWS)]
        rho = rows[6]
        square, inner, weighted = common(rows)
        double = -2.0 * tile
        zero = jnp.zeros_like(tile)
        away = jnp.where(first3, pltpu.roll(tile, ROWS - 3, 0), pltpu.roll(tile, 3, 0))
        parts = (
            (jnp.where(first3, double, 0.0), by_row(zero, r3=1.0, r6=square)),
            (jnp.where(row < 6, -away, 0.0), by_row(zero, r4=1.0, r6=inner)),
            (
                by_row(jnp.where(first3, double * rho, 0.0), r6=square),
                by_row(jnp.where(first3, double, 0.0), r3=rho, r5=1.0, r6=weighted),
            ),
        )
        for o, pair in enumerate(parts):
            for g, term in enumerate(split3(jnp.concatenate(pair, axis=0))):
                feat_ref[k, g, :, o * slots : (o + 1) * slots] = term
        high, mid, low = split3(jnp.where(first3, tile, jnp.where(row == 3, 1.0, 0.0)))
        wide = [term.astype(jnp.float32) for term in (high, mid, low)] + [zero]
        point_ref[k] = jnp.concatenate(wide, axis=0).astype(jnp.bfloat16)

    for un in range(UNROLL):
        pack_ref[idle * UNROLL + un] = far_tile
        features(idle * UNROLL + un)

    group = jnp.int32(0)
    items = jnp.int32(0)
    tallest = []
    for ty in range(ny):
        for tz in range(nz):
            layers = layers_of(tz)
            first = []
            for col in range(ncol):
                first.append(group)
                offset = group * (UNROLL * slots)
                pack_ref[group * UNROLL] = far_tile
                for dy in range(3):
                    for dz in range(3):
                        where = (col, ty + dy, layers[dz])
                        shift = by_row(0.0, r0=middle + columns[col], r1=dy - 0.5, r2=dz - 0.5)
                        at = lax.shift_right_logical(offset, slot_bits)
                        start = lax.bitwise_and(offset, slots - 1)
                        moved = pltpu.roll(src_ref[where] - shift, start, 1)
                        pack_ref[at] = jnp.where(lane < start, pack_ref[at], moved)
                        pack_ref[at + 1] = jnp.where(lane < start, moved, far_tile)
                        offset = offset + count_ref[(where[0] * tall + where[1]) * deep + where[2]]
                used = lax.shift_right_logical(offset + (slots - 1), slot_bits)
                for extra in range(UNROLL):
                    pack_ref[used + extra] = far_tile
                group = lax.div(used + (UNROLL - 1), UNROLL)
            first.append(group)
            for tx in range(nx):
                t = (tx * ny + ty) * nz + tz
                begin, end = first[ranges[tx][0]], first[ranges[tx][1]]

                def note(step, count):
                    item_ref[0, count] = t
                    item_ref[1, count] = step
                    return count + 1

                items = lax.fori_loop(begin, end, note, items)
    for extra in range(ITEMS):
        item_ref[0, items + extra] = 0
        item_ref[1, items + extra] = idle

    def build(step, carry):
        for un in range(UNROLL):
            features(step * UNROLL + un)
        return carry

    lax.fori_loop(0, group, build, 0)

    def own_of(tx, ty, tz):
        tile = own_ref[own_index(tx, ty, tz)]
        own = tile - by_row(0.0, r0=middle + tx, r1=0.5, r2=0.5)
        return tile, [own[c : c + 1] for c in range(ROWS)], own

    def own_index(tx, ty, tz):
        return tx, ty + 1, layers_of(tz)[1]

    places = [(tx, ty, tz) for tx in range(nx) for ty in range(ny) for tz in range(nz)]
    for t, place in enumerate(places):
        tile, rows, own = own_of(*place)
        square, inner, weighted = common(rows)
        second = jnp.where(first3, own * rows[6], 0.0)
        second = by_row(second, r3=square, r4=inner, r5=weighted, r6=1.0)
        terms = split3(jnp.concatenate([own, second], axis=0))
        terms = [term.astype(jnp.float32) for term in terms]
        left = jnp.concatenate([terms[g] for g in LEFT_TERMS], axis=0)
        left_ref[t] = left.T.astype(jnp.bfloat16)
        ratio_ref[t] = jnp.broadcast_to(rows[7], (slots, slots)).T
        count_ref[ncol * tall * deep + t] = live_in(tile[0:1])
    acc_ref[...] = jnp.zeros_like(acc_ref)
    sum_ref[...] = jnp.zeros_like(sum_ref)

    def ask(item, height, forms_ref):
        t, step = item_ref[0, item], item_ref[1, item]
        rights = []
        for un in range(UNROLL):
            thirds = [feat_ref[step * UNROLL + un, g] for g in range(3)]
            rights.append(jnp.concatenate([thirds[g] for g in RIGHT_TERMS], axis=0))
        forms_ref[0:height, :] = jnp.dot(
            left_ref[t, 0:height, :],
            jnp.concatenate(rights, axis=1),
            preferred_element_type=jnp.float32,
        )

    def use(item, height, forms_ref):
        t, step = item_ref[0, item], item_ref[1, item]
        pieces, dots = [], []
        change = [None] * (height // 16)
        for un in range(UNROLL):
            highs, lows = [], []
            for g in range(height // 16):
                at = slice(16 * g, 16 * g + 16)
                dist, approach, below = [
                    forms_ref[at, o * slots : (o + 1) * slots]
                    for o in range(un * FORMS, un * FORMS + FORMS)
                ]
                ratios = ratio_ref[t, at, :] + pack_ref[step * UNROLL + un, 7:8, :]
                safe = jnp.maximum(dist, 1e-30)
                radius = safe * lax.rsqrt(safe)
                if 0.5 / H_SMOOTH != 1.0:
                    radius = radius * (0.5 / H_SMOOTH)
                base = jnp.maximum(1.0 - radius, 0.0)
                weight = base * base * base
                closing = jnp.minimum(approach, 0.0) / below
                if visc != 1.0:
                    closing = closing * visc
                force = weight * (ratios - closing)
                moving = weight * approach
                change[g] = moving if change[g] is None else change[g] + moving
                high = force.astype(jnp.bfloat16)
                highs.append(high)
                lows.append((force - high.astype(jnp.float32)).astype(jnp.bfloat16))
            pieces.append(jnp.concatenate(highs, axis=0))
            pieces.append(jnp.concatenate(lows, axis=0))
            points = point_ref[step * UNROLL + un]
            dots.append(points)
            dots.append(points)
        sum_ref[t, 0:height, 0:32] += lax.dot_general(
            jnp.concatenate(pieces, axis=1),
            jnp.concatenate(dots, axis=1),
            (((1,), (1,)), ((), ())),
            preferred_element_type=jnp.float32,
        )
        for g in range(height // 16):
            acc_ref[t, 16 * g : 16 * g + 16, :] += change[g]

    ask(0, slots, even_ref)

    def visit(i, carry):
        item = ITEMS * i
        most = jnp.int32(0)
        for d in range(ITEMS + 1):
            t = item_ref[0, item + d]
            most = jnp.maximum(most, count_ref[ncol * tall * deep + t])

        def chain(height):
            for d in range(ITEMS):
                now, later = (even_ref, odd_ref) if d % 2 == 0 else (odd_ref, even_ref)
                ask(item + d + 1, height, later)
                use(item + d, height, now)

        @pl.when(most <= short)
        def _():
            chain(short)

        @pl.when(most > short)
        def _():
            chain(slots)

        return carry

    lax.fori_loop(0, lax.div(items + (ITEMS - 1), ITEMS), visit, 0)

    for t, place in enumerate(places):
        tx, ty, tz = place
        tile, rows, _ = own_of(*place)
        terms = jnp.concatenate(split3(acc_ref[t]), axis=1)
        rate = lax.dot_general(
            jnp.ones((16, 3 * slots), jnp.bfloat16),
            terms,
            (((1,), (1,)), ((), ())),
            preferred_element_type=jnp.float32,
        )[0:1]
        turned = sum_ref[t].T
        sums = turned[0:8] + turned[8:16] + turned[16:24]
        pulls = [rows[c] * sums[3:4] - sums[c : c + 1] for c in range(3)]
        if has_part:
            pulls = [pulls[c] + part_ref[place + (slice(c, c + 1),)] for c in range(3)]
            rate = rate + part_ref[place + (slice(3, 4),)]
        if not final:
            outs[0][place] = jnp.concatenate(pulls + [rate] + [jnp.zeros_like(rate)] * 4, axis=0)
            continue
        live = tile[0:1] < LIVE_BELOW
        new_vel = []
        for c in range(3):
            accel = -scale * pulls[c] + (GRAVITY if c == 2 else 0.0)
            new_vel.append(tile[3 + c : 4 + c] + TIME_STEP * accel)
        new_rho = tile[6:7] + (TIME_STEP * scale) * rate
        new_off = [tile[c : c + 1] + TIME_STEP * new_vel[c] for c in range(3)]
        if final == "last":
            off_ref, vel_ref, den_ref = outs
            for c in range(3):
                off_ref[c, tx, ty, tz, :] = jnp.where(live, new_off[c], 0.0)[0]
                vel_ref[c, tx, ty, tz, :] = jnp.where(live, new_vel[c], 0.0)[0]
            den_ref[tx, ty, tz, :] = jnp.where(live, new_rho, 0.0)[0]
        else:
            updated = jnp.concatenate(new_off + new_vel + [new_rho, ratio_of(new_rho)], axis=0)
            outs[0][place] = jnp.where(live, updated, tile)


def pair_sums(own, src, part, targets, columns, layers_of, final):
    nx, ny, nz = targets
    slots = src.shape[-1]
    ranges = []
    for tx in range(nx):
        near = [k for k, x in enumerate(columns) if abs(x - tx) <= 1]
        assert near == list(range(near[0], near[-1] + 1))
        ranges.append((near[0], near[-1] + 1))
    if final == "last":
        out_shape = (
            jax.ShapeDtypeStruct((3, nx, ny, nz, slots), jnp.float32),
            jax.ShapeDtypeStruct((3, nx, ny, nz, slots), jnp.float32),
            jax.ShapeDtypeStruct((nx, ny, nz, slots), jnp.float32),
        )
    else:
        out_shape = jax.ShapeDtypeStruct((nx, ny, nz, ROWS, slots), jnp.float32)
    kernel = functools.partial(
        pair_kernel,
        targets=targets,
        columns=columns,
        ranges=ranges,
        slots=slots,
        layers_of=layers_of,
        has_part=part is not None,
        final=final,
    )
    args = (own, src) if part is None else (own, src, part)
    vmem = pl.BlockSpec(memory_space=pltpu.VMEM)
    count = nx * ny * nz
    trips = -(-9 // UNROLL) * len(columns) * ny * nz
    tiles = (trips + 2) * UNROLL
    items = -(-9 // UNROLL) * 3 * count + 2 * ITEMS + 1
    wide = UNROLL * FORMS * slots
    return pl.pallas_call(
        kernel,
        out_shape=out_shape,
        in_specs=[vmem] * len(args),
        out_specs=jax.tree.map(lambda _: vmem, out_shape),
        scratch_shapes=[
            pltpu.VMEM((tiles, ROWS, slots), jnp.float32),
            pltpu.VMEM((tiles, 3, 16, FORMS * slots), jnp.bfloat16),
            pltpu.VMEM((tiles, 32, slots), jnp.bfloat16),
            pltpu.VMEM((count, slots, slots), jnp.bfloat16),
            pltpu.VMEM((count, slots, slots), jnp.float32),
            pltpu.VMEM((count, slots, slots), jnp.float32),
            pltpu.VMEM((slots, wide), jnp.float32),
            pltpu.VMEM((slots, wide), jnp.float32),
            pltpu.VMEM((count, slots, slots), jnp.float32),
            pltpu.SMEM((src.shape[0] * src.shape[1] * src.shape[2] + count,), jnp.int32),
            pltpu.SMEM((2, items), jnp.int32),
        ],
        compiler_params=pltpu.CompilerParams(vmem_limit_bytes=24 << 20),
    )(*args)


def per_device(offsets, velocity, density, counts):
    wide, tall, deep = offsets.shape[1:4]
    tile = pack(offsets, velocity, density, counts)

    def ends(block, dim):
        size = block.shape[dim]
        first = lax.slice_in_dim(block, 0, 1, axis=dim)
        return first, lax.slice_in_dim(block, size - 1, size, axis=dim)

    def with_layers(block):
        first, last = ends(block, 2)
        if lax.axis_size("gz") == 1:
            return block, lambda z: z % deep
        if lax.axis_size("gz") * deep == 2:
            return jnp.concatenate([block, from_after(first, "gz")], axis=2), lambda z: z % 2
        size = lax.axis_size("gz")
        parts = [block, from_after(first, "gz"), from_after(last, "gz", size - 1)]
        return jnp.concatenate(parts, axis=2), lambda z: z % (deep + 2)

    def with_rows(block):
        before, after = neighbours(*ends(block, 1), "gy")
        return jnp.concatenate([before, block, after], axis=1)

    targets = (wide, tall, deep)
    assert wide >= 2

    block, layer = with_layers(tile)
    own = with_rows(block)
    layers_of = lambda z: (layer(z - 1), layer(z), layer(z + 1))
    before, after = neighbours(*ends(own, 0), "gx")
    src = jnp.concatenate([before, own, after], axis=0)
    columns = tuple(range(-1, wide + 1))
    state = pair_sums(own, src, None, targets, columns, layers_of, "step")

    block, layer = with_layers(state)
    own = with_rows(block)
    src = jnp.concatenate([own, from_after(own[0:2], "gx")], axis=0)
    return pair_sums(src[1 : wide + 1], src, None, targets, columns, layers_of, "last")


def solution(mesh):
    return jax.shard_map(
        per_device,
        mesh=mesh,
        in_specs=(
            P(None, "gx", "gy", "gz", None),
            P(None, "gx", "gy", "gz", None),
            P("gx", "gy", "gz", None),
            P("gx", "gy", "gz"),
        ),
        out_specs=(
            P(None, "gx", "gy", "gz", None),
            P(None, "gx", "gy", "gz", None),
            P("gx", "gy", "gz", None),
        ),
        check_vma=False,
    )
```

```python
import functools
import math

import jax
import jax.numpy as jnp
from jax import lax
from jax.experimental import pallas as pl
from jax.experimental.pallas import tpu as pltpu
from jax.sharding import PartitionSpec as P

H_SMOOTH = 0.5
KERNEL_NORM = 21.0 / (16.0 * math.pi * H_SMOOTH**3)
SOUND_SPEED = 10.0
STIFFNESS = SOUND_SPEED * SOUND_SPEED / 7.0
VISC_ALPHA = 0.1
TIME_STEP = 0.01
GRAVITY = -2.0
FAR = 1000.0
LIVE_BELOW = 500.0
ROWS = 8
UNROLL = 3
FORMS = 3


def ratio_of(rho):
    square = rho * rho
    return STIFFNESS * (square * square * square * rho - 1.0) / square


def pack(offsets, velocity, density, counts):
    wide, tall, deep, slots = density.shape

    def kernel(off_any, vel_any, den_any, count_ref, out_ref, off_ref, vel_ref, den_ref, sems):
        copies = [
            pltpu.make_async_copy(off_any, off_ref, sems.at[0]),
            pltpu.make_async_copy(vel_any, vel_ref, sems.at[1]),
            pltpu.make_async_copy(den_any, den_ref, sems.at[2]),
        ]
        for copy in copies:
            copy.start()
        for copy in copies:
            copy.wait()
        lane = lax.broadcasted_iota(jnp.int32, (1, slots), 1)
        for a in range(wide):
            for b in range(tall):
                for c in range(deep):
                    live = lane < count_ref[a, c, b]
                    rho = den_ref[a, b, c].reshape(1, slots)
                    rows = [ref[d, a, b, c].reshape(1, slots) for ref in (off_ref, vel_ref) for d in range(3)]
                    rows[0] = jnp.where(live, rows[0], FAR)
                    out_ref[a, b, c] = jnp.concatenate(rows + [rho, ratio_of(rho)], axis=0)

    whole = pl.BlockSpec(memory_space=pl.ANY)
    return pl.pallas_call(
        kernel,
        out_shape=jax.ShapeDtypeStruct((wide, tall, deep, ROWS, slots), jnp.float32),
        in_specs=[whole, whole, whole, pl.BlockSpec(memory_space=pltpu.SMEM)],
        out_specs=pl.BlockSpec(memory_space=pltpu.VMEM),
        scratch_shapes=[
            pltpu.VMEM(offsets.shape, jnp.float32),
            pltpu.VMEM(velocity.shape, jnp.float32),
            pltpu.VMEM(density.shape, jnp.float32),
            pltpu.SemaphoreType.DMA((3,)),
        ],
    )(offsets, velocity, density, jnp.swapaxes(counts, 1, 2))


def neighbours(first, last, axis):
    size = lax.axis_size(axis)
    even = lax.axis_index(axis) % 2 == 0
    ones = [(i, i ^ 1) for i in range(size)]
    twos = [(i, ((i + 1) ^ 1) - 1) for i in range(size)]
    twos = [(i, j % size) for i, j in twos]
    got_two = lax.ppermute(jnp.where(even, first, last), axis, twos)
    got_one = lax.ppermute(jnp.where(even, last, first), axis, ones)
    before = jnp.where(even, got_two, got_one)
    after = jnp.where(even, got_one, got_two)
    return before, after


def from_after(value, axis, steps=1):
    size = lax.axis_size(axis)
    return lax.ppermute(value, axis, [((i + steps) % size, i) for i in range(size)])


def split3(value):
    high = value.astype(jnp.bfloat16)
    rest = value - high.astype(jnp.float32)
    middle = rest.astype(jnp.bfloat16)
    low = (rest - middle.astype(jnp.float32)).astype(jnp.bfloat16)
    return high, middle, low


LEFT_TERMS = (0, 0, 0, 1, 1, 2, 1, 2)
RIGHT_TERMS = (0, 1, 2, 0, 1, 0, 2, 1)


def pair_kernel(*refs, targets, columns, ranges, slots, layers_of, has_part, final, chain):
    own_ref, src_ref = refs[:2]
    part_ref = refs[2] if has_part else None
    outs = refs[2 + has_part : -11]
    pack_ref, feat_ref, point_ref, left_ref, acc_ref, sum_ref = refs[-11:-5]
    even_ref, odd_ref, ratio_ref, count_ref, item_ref = refs[-5:]
    nx, ny, nz = targets
    tall, deep = src_ref.shape[1:3]
    ncol = len(columns)
    row = lax.broadcasted_iota(jnp.int32, (ROWS, slots), 0)
    lane = lax.broadcasted_iota(jnp.int32, (ROWS, slots), 1)
    far_tile = jnp.where(row == 0, FAR, 0.0)
    first3 = row < 3
    eps = 0.01 * H_SMOOTH * H_SMOOTH
    visc = 2.0 * VISC_ALPHA * SOUND_SPEED * H_SMOOTH
    particle_mass = 2.0 / slots
    scale = particle_mass * (-5.0 * KERNEL_NORM / (H_SMOOTH * H_SMOOTH))
    middle = 1.0 - 0.5 * nx
    slot_bits = slots.bit_length() - 1
    assert slots == 1 << slot_bits
    short = (3 * slots) // 4
    idle = feat_ref.shape[0] // UNROLL - 1

    def live_in(tile_row):
        return jnp.sum(jnp.where(tile_row < LIVE_BELOW, 1, 0))

    for a in range(ncol):
        for b in range(tall):
            for c in range(deep):
                count_ref[(a * tall + b) * deep + c] = live_in(src_ref[a, b, c, 0:1])

    def by_row(default, **kinds):
        result = default
        for name, value in kinds.items():
            result = jnp.where(row == int(name[1:]), value, result)
        return result

    def common(rows):
        x, y, z, u, v, w, rho, _ = rows
        square = x * x + y * y + z * z
        inner = u * x + v * y + w * z
        return square, inner, rho * (square + eps)

    def features(k):
        tile = pack_ref[k]
        rows = [pack_ref[k, c : c + 1, :] for c in range(ROWS)]
        rho = rows[6]
        square, inner, weighted = common(rows)
        double = -2.0 * tile
        zero = jnp.zeros_like(tile)
        away = jnp.where(first3, pltpu.roll(tile, ROWS - 3, 0), pltpu.roll(tile, 3, 0))
        parts = (
            (jnp.where(first3, double, 0.0), by_row(zero, r3=1.0, r6=square)),
            (jnp.where(row < 6, -away, 0.0), by_row(zero, r4=1.0, r6=inner)),
            (
                by_row(jnp.where(first3, double * rho, 0.0), r6=square),
                by_row(jnp.where(first3, double, 0.0), r3=rho, r5=1.0, r6=weighted),
            ),
        )
        for o, pair in enumerate(parts):
            for g, term in enumerate(split3(jnp.concatenate(pair, axis=0))):
                feat_ref[k, g, :, o * slots : (o + 1) * slots] = term
        high, mid, low = split3(jnp.where(first3, tile, jnp.where(row == 3, 1.0, 0.0)))
        wide = [term.astype(jnp.float32) for term in (high, mid, low)] + [zero]
        point_ref[k] = jnp.concatenate(wide, axis=0).astype(jnp.bfloat16)

    for un in range(UNROLL):
        pack_ref[idle * UNROLL + un] = far_tile
        features(idle * UNROLL + un)

    group = jnp.int32(0)
    items = jnp.int32(0)
    tallest = []
    for ty in range(ny):
        for tz in range(nz):
            layers = layers_of(tz)
            first = []
            for col in range(ncol):
                first.append(group)
                offset = group * (UNROLL * slots)
                pack_ref[group * UNROLL] = far_tile
                for dy in range(3):
                    for dz in range(3):
                        where = (col, ty + dy, layers[dz])
                        shift = by_row(0.0, r0=middle + columns[col], r1=dy - 0.5, r2=dz - 0.5)
                        at = lax.shift_right_logical(offset, slot_bits)
                        start = lax.bitwise_and(offset, slots - 1)
                        moved = pltpu.roll(src_ref[where] - shift, start, 1)
                        pack_ref[at] = jnp.where(lane < start, pack_ref[at], moved)
                        pack_ref[at + 1] = jnp.where(lane < start, moved, far_tile)
                        offset = offset + count_ref[(where[0] * tall + where[1]) * deep + where[2]]
                used = lax.shift_right_logical(offset + (slots - 1), slot_bits)
                for extra in range(UNROLL):
                    pack_ref[used + extra] = far_tile
                group = lax.div(used + (UNROLL - 1), UNROLL)
            first.append(group)
            for tx in range(nx):
                t = (tx * ny + ty) * nz + tz
                begin, end = first[ranges[tx][0]], first[ranges[tx][1]]

                def note(step, count):
                    item_ref[0, count] = t
                    item_ref[1, count] = step
                    return count + 1

                items = lax.fori_loop(begin, end, note, items)
    for extra in range(2):
        item_ref[0, items + extra] = 0
        item_ref[1, items + extra] = idle

    def build(step, carry):
        for un in range(UNROLL):
            features(step * UNROLL + un)
        return carry

    lax.fori_loop(0, group, build, 0)

    def own_of(tx, ty, tz):
        tile = own_ref[own_index(tx, ty, tz)]
        own = tile - by_row(0.0, r0=middle + tx, r1=0.5, r2=0.5)
        return tile, [own[c : c + 1] for c in range(ROWS)], own

    def own_index(tx, ty, tz):
        return tx, ty + 1, layers_of(tz)[1]

    places = [(tx, ty, tz) for tx in range(nx) for ty in range(ny) for tz in range(nz)]
    for t, place in enumerate(places):
        tile, rows, own = own_of(*place)
        square, inner, weighted = common(rows)
        second = jnp.where(first3, own * rows[6], 0.0)
        second = by_row(second, r3=square, r4=inner, r5=weighted, r6=1.0)
        terms = split3(jnp.concatenate([own, second], axis=0))
        terms = [term.astype(jnp.float32) for term in terms]
        left = jnp.concatenate([terms[g] for g in LEFT_TERMS], axis=0)
        left_ref[t] = left.T.astype(jnp.bfloat16)
        ratio_ref[t] = jnp.broadcast_to(rows[7], (slots, slots)).T
        count_ref[ncol * tall * deep + t] = live_in(tile[0:1])
    acc_ref[...] = jnp.zeros_like(acc_ref)
    sum_ref[...] = jnp.zeros_like(sum_ref)

    def ask(item, height, forms_ref):
        t, step = item_ref[0, item], item_ref[1, item]
        rights = []
        for un in range(UNROLL):
            thirds = [feat_ref[step * UNROLL + un, g] for g in range(3)]
            rights.append(jnp.concatenate([thirds[g] for g in RIGHT_TERMS], axis=0))
        forms_ref[0:height, :] = jnp.dot(
            left_ref[t, 0:height, :],
            jnp.concatenate(rights, axis=1),
            preferred_element_type=jnp.float32,
        )

    def use(item, height, forms_ref):
        t, step = item_ref[0, item], item_ref[1, item]
        pieces, dots = [], []
        change = [None] * (height // 16)
        for un in range(UNROLL):
            highs, lows = [], []
            for g in range(height // 16):
                at = slice(16 * g, 16 * g + 16)
                dist, approach, below = [
                    forms_ref[at, o * slots : (o + 1) * slots]
                    for o in range(un * FORMS, un * FORMS + FORMS)
                ]
                ratios = ratio_ref[t, at, :] + pack_ref[step * UNROLL + un, 7:8, :]
                safe = jnp.maximum(dist, 1e-30)
                radius = safe * lax.rsqrt(safe)
                if 0.5 / H_SMOOTH != 1.0:
                    radius = radius * (0.5 / H_SMOOTH)
                base = jnp.maximum(1.0 - radius, 0.0)
                weight = base * base * base
                closing = jnp.minimum(approach, 0.0) / below
                if visc != 1.0:
                    closing = closing * visc
                force = weight * (ratios - closing)
                moving = weight * approach
                change[g] = moving if change[g] is None else change[g] + moving
                high = force.astype(jnp.bfloat16)
                highs.append(high)
                lows.append((force - high.astype(jnp.float32)).astype(jnp.bfloat16))
            pieces.append(jnp.concatenate(highs, axis=0))
            pieces.append(jnp.concatenate(lows, axis=0))
            points = point_ref[step * UNROLL + un]
            dots.append(points)
            dots.append(points)
        sum_ref[t, 0:height, 0:32] += lax.dot_general(
            jnp.concatenate(pieces, axis=1),
            jnp.concatenate(dots, axis=1),
            (((1,), (1,)), ((), ())),
            preferred_element_type=jnp.float32,
        )
        for g in range(height // 16):
            acc_ref[t, 16 * g : 16 * g + 16, :] += change[g]

    ask(0, slots, even_ref)

    def visits(length, origin, count):
        def visit(i, carry):
            item = origin + length * i
            most = jnp.int32(0)
            for d in range(length + 1):
                t = item_ref[0, item + d]
                most = jnp.maximum(most, count_ref[ncol * tall * deep + t])

            def steps(height):
                for d in range(length):
                    now, later = (even_ref, odd_ref) if d % 2 == 0 else (odd_ref, even_ref)
                    ask(item + d + 1, height, later)
                    use(item + d, height, now)

            @pl.when(most <= short)
            def _():
                steps(short)

            @pl.when(most > short)
            def _():
                steps(slots)

            return carry

        lax.fori_loop(0, count, visit, 0)

    chains = lax.div(items, chain)
    visits(chain, 0, chains)
    visits(2, chains * chain, lax.div(items - chains * chain + 1, 2))

    for t, place in enumerate(places):
        tx, ty, tz = place
        tile, rows, _ = own_of(*place)
        terms = jnp.concatenate(split3(acc_ref[t]), axis=1)
        rate = lax.dot_general(
            jnp.ones((16, 3 * slots), jnp.bfloat16),
            terms,
            (((1,), (1,)), ((), ())),
            preferred_element_type=jnp.float32,
        )[0:1]
        turned = sum_ref[t].T
        sums = turned[0:8] + turned[8:16] + turned[16:24]
        pulls = [rows[c] * sums[3:4] - sums[c : c + 1] for c in range(3)]
        if has_part and tx < part_ref.shape[0]:
            pulls = [pulls[c] + part_ref[place + (slice(c, c + 1),)] for c in range(3)]
            rate = rate + part_ref[place + (slice(3, 4),)]
        if not final:
            outs[0][place] = jnp.concatenate(pulls + [rate] + [jnp.zeros_like(rate)] * 4, axis=0)
            continue
        live = tile[0:1] < LIVE_BELOW
        new_vel = []
        for c in range(3):
            accel = -scale * pulls[c] + (GRAVITY if c == 2 else 0.0)
            new_vel.append(tile[3 + c : 4 + c] + TIME_STEP * accel)
        new_rho = tile[6:7] + (TIME_STEP * scale) * rate
        new_off = [tile[c : c + 1] + TIME_STEP * new_vel[c] for c in range(3)]
        if final == "last":
            off_ref, vel_ref, den_ref = outs
            for c in range(3):
                off_ref[c, tx, ty, tz, :] = jnp.where(live, new_off[c], 0.0)[0]
                vel_ref[c, tx, ty, tz, :] = jnp.where(live, new_vel[c], 0.0)[0]
            den_ref[tx, ty, tz, :] = jnp.where(live, new_rho, 0.0)[0]
        else:
            updated = jnp.concatenate(new_off + new_vel + [new_rho, ratio_of(new_rho)], axis=0)
            outs[0][place] = jnp.where(live, updated, tile)


def pair_sums(own, src, part, targets, columns, layers_of, final, chain=6, skip=()):
    nx, ny, nz = targets
    slots = src.shape[-1]
    ranges = []
    for tx in range(nx):
        near = [k for k, x in enumerate(columns) if abs(x - tx) <= 1 and (tx, x) not in skip]
        near = near or [0, -1]
        assert near == list(range(near[0], near[-1] + 1)) or near == [0, -1]
        ranges.append((near[0], near[-1] + 1))
    if final == "last":
        out_shape = (
            jax.ShapeDtypeStruct((3, nx, ny, nz, slots), jnp.float32),
            jax.ShapeDtypeStruct((3, nx, ny, nz, slots), jnp.float32),
            jax.ShapeDtypeStruct((nx, ny, nz, slots), jnp.float32),
        )
    else:
        out_shape = jax.ShapeDtypeStruct((nx, ny, nz, ROWS, slots), jnp.float32)
    kernel = functools.partial(
        pair_kernel,
        targets=targets,
        columns=columns,
        ranges=ranges,
        slots=slots,
        layers_of=layers_of,
        has_part=part is not None,
        final=final,
        chain=chain,
    )
    args = (own, src) if part is None else (own, src, part)
    vmem = pl.BlockSpec(memory_space=pltpu.VMEM)
    count = nx * ny * nz
    trips = -(-9 // UNROLL) * len(columns) * ny * nz
    tiles = (trips + 2) * UNROLL
    items = -(-9 // UNROLL) * 3 * count + 2 * chain + 1
    wide = UNROLL * FORMS * slots
    return pl.pallas_call(
        kernel,
        out_shape=out_shape,
        in_specs=[vmem] * len(args),
        out_specs=jax.tree.map(lambda _: vmem, out_shape),
        scratch_shapes=[
            pltpu.VMEM((tiles, ROWS, slots), jnp.float32),
            pltpu.VMEM((tiles, 3, 16, FORMS * slots), jnp.bfloat16),
            pltpu.VMEM((tiles, 32, slots), jnp.bfloat16),
            pltpu.VMEM((count, slots, slots), jnp.bfloat16),
            pltpu.VMEM((count, slots, slots), jnp.float32),
            pltpu.VMEM((count, slots, slots), jnp.float32),
            pltpu.VMEM((slots, wide), jnp.float32),
            pltpu.VMEM((slots, wide), jnp.float32),
            pltpu.VMEM((count, slots, slots), jnp.float32),
            pltpu.SMEM((src.shape[0] * src.shape[1] * src.shape[2] + count,), jnp.int32),
            pltpu.SMEM((2, items), jnp.int32),
        ],
        compiler_params=pltpu.CompilerParams(vmem_limit_bytes=24 << 20),
        cost_estimate=pl.CostEstimate(
            flops=count * 9 * len(columns) * slots * slots * 40, bytes_accessed=src.size * 4, transcendentals=0
        ),
    )(*args)


def per_device(offsets, velocity, density, counts):
    wide, tall, deep = offsets.shape[1:4]
    tile = pack(offsets, velocity, density, counts)

    def ends(block, dim):
        size = block.shape[dim]
        first = lax.slice_in_dim(block, 0, 1, axis=dim)
        return first, lax.slice_in_dim(block, size - 1, size, axis=dim)

    def with_layers(block):
        first, last = ends(block, 2)
        if lax.axis_size("gz") == 1:
            return block, lambda z: z % deep
        if lax.axis_size("gz") * deep == 2:
            return jnp.concatenate([block, from_after(first, "gz")], axis=2), lambda z: z % 2
        size = lax.axis_size("gz")
        parts = [block, from_after(first, "gz"), from_after(last, "gz", size - 1)]
        return jnp.concatenate(parts, axis=2), lambda z: z % (deep + 2)

    def with_rows(block):
        before, after = neighbours(*ends(block, 1), "gy")
        return jnp.concatenate([before, block, after], axis=1)

    targets = (wide, tall, deep)
    assert wide >= 2

    block, layer = with_layers(tile)
    own = with_rows(block)
    layers_of = lambda z: (layer(z - 1), layer(z), layer(z + 1))
    before, after = neighbours(*ends(own, 0), "gx")
    inside = pair_sums(own, own, None, targets, tuple(range(wide)), layers_of, None)
    outside = jnp.concatenate([before, after], axis=0)
    state = pair_sums(own, outside, inside, targets, (-1, wide), layers_of, "step", chain=4)

    block, layer = with_layers(state)
    own = with_rows(block)
    next_two = from_after(own[0:2], "gx")
    here = tuple(range(-1, wide - 1))
    inside = pair_sums(
        own[1:], own, None, (wide - 1, tall, deep), here, layers_of, None, chain=4
    )
    done = {(tx, x) for tx in range(wide - 1) for x in here}
    src = jnp.concatenate([own[1:], next_two], axis=0)
    columns = tuple(range(0, wide + 1))
    return pair_sums(src[:wide], src, inside, targets, columns, layers_of, "last", skip=done)


def solution(mesh):
    return jax.shard_map(
        per_device,
        mesh=mesh,
        in_specs=(
            P(None, "gx", "gy", "gz", None),
            P(None, "gx", "gy", "gz", None),
            P("gx", "gy", "gz", None),
            P("gx", "gy", "gz"),
        ),
        out_specs=(
            P(None, "gx", "gy", "gz", None),
            P(None, "gx", "gy", "gz", None),
            P("gx", "gy", "gz", None),
        ),
        check_vma=False,
    )
```

```python
import functools
import math

import jax
import jax.numpy as jnp
from jax import lax
from jax.experimental import pallas as pl
from jax.experimental.pallas import tpu as pltpu
from jax.sharding import PartitionSpec as P

H_SMOOTH = 0.5
KERNEL_NORM = 21.0 / (16.0 * math.pi * H_SMOOTH**3)
SOUND_SPEED = 10.0
STIFFNESS = SOUND_SPEED * SOUND_SPEED / 7.0
VISC_ALPHA = 0.1
TIME_STEP = 0.01
GRAVITY = -2.0
FAR = 1000.0
LIVE_BELOW = 500.0
ROWS = 8
UNROLL = 3
FORMS = 3


def ratio_of(rho):
    square = rho * rho
    return STIFFNESS * (square * square * square * rho - 1.0) / square


def pack(offsets, velocity, density, counts):
    wide, tall, deep, slots = density.shape

    def kernel(off_any, vel_any, den_any, count_any, out_ref, off_ref, vel_ref, den_ref, count_ref, sems):
        copies = [
            pltpu.make_async_copy(off_any, off_ref, sems.at[0]),
            pltpu.make_async_copy(vel_any, vel_ref, sems.at[1]),
            pltpu.make_async_copy(den_any, den_ref, sems.at[2]),
            pltpu.make_async_copy(count_any, count_ref, sems.at[3]),
        ]
        for copy in copies:
            copy.start()
        for copy in copies:
            copy.wait()
        lane = lax.broadcasted_iota(jnp.int32, (1, slots), 1)
        for a in range(wide):
            for b in range(tall):
                for c in range(deep):
                    live = lane < count_ref[a, c, b]
                    count = jnp.full((1, slots), count_ref[a, c, b].astype(jnp.float32))
                    rho = den_ref[a, b, c].reshape(1, slots)
                    rows = [ref[d, a, b, c].reshape(1, slots) for ref in (off_ref, vel_ref) for d in range(3)]
                    rows[0] = jnp.where(live, rows[0], FAR)
                    out_ref[a, b, c] = jnp.concatenate(rows + [rho, count], axis=0)

    whole = pl.BlockSpec(memory_space=pl.ANY)
    return pl.pallas_call(
        kernel,
        out_shape=jax.ShapeDtypeStruct((wide, tall, deep, ROWS, slots), jnp.float32),
        in_specs=[whole] * 4,
        out_specs=pl.BlockSpec(memory_space=pltpu.VMEM),
        scratch_shapes=[
            pltpu.VMEM(offsets.shape, jnp.float32),
            pltpu.VMEM(velocity.shape, jnp.float32),
            pltpu.VMEM(density.shape, jnp.float32),
            pltpu.SMEM((wide, deep, tall), jnp.int32),
            pltpu.SemaphoreType.DMA((4,)),
        ],
    )(offsets, velocity, density, jnp.swapaxes(counts, 1, 2))


def neighbours(first, last, axis):
    size = lax.axis_size(axis)
    even = lax.axis_index(axis) % 2 == 0
    ones = [(i, i ^ 1) for i in range(size)]
    twos = [(i, ((i + 1) ^ 1) - 1) for i in range(size)]
    twos = [(i, j % size) for i, j in twos]
    got_two = lax.ppermute(jnp.where(even, first, last), axis, twos)
    got_one = lax.ppermute(jnp.where(even, last, first), axis, ones)
    before = jnp.where(even, got_two, got_one)
    after = jnp.where(even, got_one, got_two)
    return before, after


def from_after(value, axis, steps=1):
    size = lax.axis_size(axis)
    return lax.ppermute(value, axis, [((i + steps) % size, i) for i in range(size)])


def split3(value):
    high = value.astype(jnp.bfloat16)
    rest = value - high.astype(jnp.float32)
    middle = rest.astype(jnp.bfloat16)
    low = (rest - middle.astype(jnp.float32)).astype(jnp.bfloat16)
    return high, middle, low


LEFT_TERMS = (0, 0, 0, 1, 1, 2, 1, 2)
RIGHT_TERMS = (0, 1, 2, 0, 1, 0, 2, 1)


def pair_kernel(*refs, targets, columns, ranges, slots, layers_of, has_part, final, chain):
    own_ref, src_ref = refs[:2]
    part_ref = refs[2] if has_part else None
    outs = refs[2 + has_part : -11]
    pack_ref, feat_ref, point_ref, left_ref, acc_ref, sum_ref = refs[-11:-5]
    even_ref, odd_ref, ratio_ref, count_ref, item_ref = refs[-5:]
    nx, ny, nz = targets
    tall, deep = src_ref.shape[1:3]
    ncol = len(columns)
    row = lax.broadcasted_iota(jnp.int32, (ROWS, slots), 0)
    lane = lax.broadcasted_iota(jnp.int32, (ROWS, slots), 1)
    far_tile = jnp.where(row == 0, FAR, jnp.where(row == 6, 1.0, 0.0))
    first3 = row < 3
    eps = 0.01 * H_SMOOTH * H_SMOOTH
    visc = 2.0 * VISC_ALPHA * SOUND_SPEED * H_SMOOTH
    particle_mass = 2.0 / slots
    scale = particle_mass * (-5.0 * KERNEL_NORM / (H_SMOOTH * H_SMOOTH))
    middle = 1.0 - 0.5 * nx
    slot_bits = slots.bit_length() - 1
    assert slots == 1 << slot_bits
    short = (3 * slots) // 4
    idle = feat_ref.shape[0] // UNROLL - 1
    most_trips = -(-9 // UNROLL)

    def live_in(tile_row):
        return tile_row[0, 0].astype(jnp.int32)

    for a in range(ncol):
        for b in range(tall):
            for c in range(deep):
                count_ref[(a * tall + b) * deep + c] = live_in(src_ref[a, b, c, 7:8])

    def by_row(default, **kinds):
        result = default
        for name, value in kinds.items():
            result = jnp.where(row == int(name[1:]), value, result)
        return result

    def common(rows):
        x, y, z, u, v, w, rho, _ = rows
        square = x * x + y * y + z * z
        inner = u * x + v * y + w * z
        return square, inner, rho * (square + eps)

    def features(k):
        tile = pack_ref[k]
        rows = [pack_ref[k, c : c + 1, :] for c in range(ROWS)]
        rho = rows[6]
        square, inner, weighted = common(rows)
        double = -2.0 * tile
        zero = jnp.zeros_like(tile)
        away = jnp.where(first3, pltpu.roll(tile, ROWS - 3, 0), pltpu.roll(tile, 3, 0))
        parts = (
            (jnp.where(first3, double, 0.0), by_row(zero, r3=1.0, r6=square)),
            (jnp.where(row < 6, -away, 0.0), by_row(zero, r4=1.0, r6=inner)),
            (
                by_row(jnp.where(first3, double * rho, 0.0), r6=square),
                by_row(jnp.where(first3, double, 0.0), r3=rho, r5=1.0, r6=weighted),
            ),
        )
        for o, pair in enumerate(parts):
            for g, term in enumerate(split3(jnp.concatenate(pair, axis=0))):
                feat_ref[k, g, :, o * slots : (o + 1) * slots] = term
        pack_ref[k, 7:8, :] = ratio_of(rho)
        high, mid, low = split3(jnp.where(first3, tile, jnp.where(row == 3, 1.0, 0.0)))
        wide = [term.astype(jnp.float32) for term in (high, mid, low)] + [zero]
        point_ref[k] = jnp.concatenate(wide, axis=0).astype(jnp.bfloat16)

    for un in range(UNROLL):
        pack_ref[idle * UNROLL + un] = far_tile
        features(idle * UNROLL + un)

    def own_of(tx, ty, tz):
        tile = own_ref[own_index(tx, ty, tz)]
        own = tile - by_row(0.0, r0=middle + tx, r1=0.5, r2=0.5)
        return tile, [own[c : c + 1] for c in range(ROWS)], own

    def own_index(tx, ty, tz):
        return tx, ty + 1, layers_of(tz)[1]

    places = [(tx, ty, tz) for tx in range(nx) for ty in range(ny) for tz in range(nz)]
    for t, place in enumerate(places):
        tile, rows, own = own_of(*place)
        square, inner, weighted = common(rows)
        second = jnp.where(first3, own * rows[6], 0.0)
        second = by_row(second, r3=square, r4=inner, r5=weighted, r6=1.0)
        terms = split3(jnp.concatenate([own, second], axis=0))
        terms = [term.astype(jnp.float32) for term in terms]
        left = jnp.concatenate([terms[g] for g in LEFT_TERMS], axis=0)
        left_ref[t] = left.T.astype(jnp.bfloat16)
        ratio_ref[t] = jnp.broadcast_to(ratio_of(rows[6]), (slots, slots)).T
        count_ref[ncol * tall * deep + t] = live_in(tile[7:8])
    acc_ref[...] = jnp.zeros_like(acc_ref)
    sum_ref[...] = jnp.zeros_like(sum_ref)

    group = jnp.int32(0)
    items = jnp.int32(0)
    tallest = []
    for ty in range(ny):
        for tz in range(nz):
            layers = layers_of(tz)
            first = []
            for col in range(ncol):
                first.append(group)
                offset = group * (UNROLL * slots)
                pack_ref[group * UNROLL] = far_tile
                for dy in range(3):
                    for dz in range(3):
                        where = (col, ty + dy, layers[dz])
                        shift = by_row(0.0, r0=middle + columns[col], r1=dy - 0.5, r2=dz - 0.5)
                        at = lax.shift_right_logical(offset, slot_bits)
                        start = lax.bitwise_and(offset, slots - 1)
                        moved = pltpu.roll(src_ref[where] - shift, start, 1)
                        pack_ref[at] = jnp.where(lane < start, pack_ref[at], moved)
                        pack_ref[at + 1] = jnp.where(lane < start, moved, far_tile)
                        offset = offset + count_ref[(where[0] * tall + where[1]) * deep + where[2]]
                used = lax.shift_right_logical(offset + (slots - 1), slot_bits)
                for extra in range(UNROLL):
                    pack_ref[used + extra] = far_tile
                group = lax.div(used + (UNROLL - 1), UNROLL)
            first.append(group)
            for tx in range(nx):
                t = (tx * ny + ty) * nz + tz
                begin, end = first[ranges[tx][0]], first[ranges[tx][1]]
                for k in range(most_trips * (ranges[tx][1] - ranges[tx][0])):
                    item_ref[0, items + k] = t
                    item_ref[1, items + k] = begin + k
                items = items + (end - begin)
    for extra in range(2):
        item_ref[0, items + extra] = 0
        item_ref[1, items + extra] = idle

    def build(step, carry):
        for un in range(UNROLL):
            features(step * UNROLL + un)
        return carry

    lax.fori_loop(0, group, build, 0)

    def ask(item, height, forms_ref):
        t, step = item_ref[0, item], item_ref[1, item]
        rights = []
        for un in range(UNROLL):
            thirds = [feat_ref[step * UNROLL + un, g] for g in range(3)]
            rights.append(jnp.concatenate([thirds[g] for g in RIGHT_TERMS], axis=0))
        forms_ref[0:height, :] = jnp.dot(
            left_ref[t, 0:height, :],
            jnp.concatenate(rights, axis=1),
            preferred_element_type=jnp.float32,
        )

    def use(item, height, forms_ref):
        t, step = item_ref[0, item], item_ref[1, item]
        pieces, dots = [], []
        change = [None] * (height // 16)
        for un in range(UNROLL):
            highs, lows = [], []
            for g in range(height // 16):
                at = slice(16 * g, 16 * g + 16)
                dist, approach, below = [
                    forms_ref[at, o * slots : (o + 1) * slots]
                    for o in range(un * FORMS, un * FORMS + FORMS)
                ]
                ratios = ratio_ref[t, at, :] + pack_ref[step * UNROLL + un, 7:8, :]
                safe = jnp.maximum(dist, 1e-30)
                radius = safe * lax.rsqrt(safe)
                if 0.5 / H_SMOOTH != 1.0:
                    radius = radius * (0.5 / H_SMOOTH)
                base = jnp.maximum(1.0 - radius, 0.0)
                weight = base * base * base
                closing = jnp.minimum(approach, 0.0) / below
                if visc != 1.0:
                    closing = closing * visc
                force = weight * (ratios - closing)
                moving = weight * approach
                change[g] = moving if change[g] is None else change[g] + moving
                high = force.astype(jnp.bfloat16)
                highs.append(high)
                lows.append((force - high.astype(jnp.float32)).astype(jnp.bfloat16))
            pieces.append(jnp.concatenate(highs, axis=0))
            pieces.append(jnp.concatenate(lows, axis=0))
            points = point_ref[step * UNROLL + un]
            dots.append(points)
            dots.append(points)
        sum_ref[t, 0:height, 0:32] += lax.dot_general(
            jnp.concatenate(pieces, axis=1),
            jnp.concatenate(dots, axis=1),
            (((1,), (1,)), ((), ())),
            preferred_element_type=jnp.float32,
        )
        for g in range(height // 16):
            acc_ref[t, 16 * g : 16 * g + 16, :] += change[g]

    ask(0, slots, even_ref)

    def visits(length, origin, count):
        def visit(i, carry):
            item = origin + length * i
            most = jnp.int32(0)
            for d in range(length + 1):
                t = item_ref[0, item + d]
                most = jnp.maximum(most, count_ref[ncol * tall * deep + t])

            def steps(height):
                for d in range(length):
                    now, later = (even_ref, odd_ref) if d % 2 == 0 else (odd_ref, even_ref)
                    ask(item + d + 1, height, later)
                    use(item + d, height, now)

            @pl.when(most <= short)
            def _():
                steps(short)

            @pl.when(most > short)
            def _():
                steps(slots)

            return carry

        lax.fori_loop(0, count, visit, 0)

    chains = lax.div(items, chain)
    visits(chain, 0, chains)
    visits(2, chains * chain, lax.div(items - chains * chain + 1, 2))

    for t, place in enumerate(places):
        tx, ty, tz = place
        tile, rows, _ = own_of(*place)
        terms = jnp.concatenate(split3(acc_ref[t]), axis=1)
        rate = lax.dot_general(
            jnp.ones((16, 3 * slots), jnp.bfloat16),
            terms,
            (((1,), (1,)), ((), ())),
            preferred_element_type=jnp.float32,
        )[0:1]
        turned = sum_ref[t].T
        sums = turned[0:8] + turned[8:16] + turned[16:24]
        pulls = [rows[c] * sums[3:4] - sums[c : c + 1] for c in range(3)]
        if has_part and tx < part_ref.shape[0]:
            pulls = [pulls[c] + part_ref[place + (slice(c, c + 1),)] for c in range(3)]
            rate = rate + part_ref[place + (slice(3, 4),)]
        if not final:
            outs[0][place] = jnp.concatenate(pulls + [rate] + [jnp.zeros_like(rate)] * 4, axis=0)
            continue
        live = tile[0:1] < LIVE_BELOW
        new_vel = []
        for c in range(3):
            accel = -scale * pulls[c] + (GRAVITY if c == 2 else 0.0)
            new_vel.append(tile[3 + c : 4 + c] + TIME_STEP * accel)
        new_rho = tile[6:7] + (TIME_STEP * scale) * rate
        new_off = [tile[c : c + 1] + TIME_STEP * new_vel[c] for c in range(3)]
        if final == "last":
            off_ref, vel_ref, den_ref = outs
            for c in range(3):
                off_ref[c, tx, ty, tz, :] = jnp.where(live, new_off[c], 0.0)[0]
                vel_ref[c, tx, ty, tz, :] = jnp.where(live, new_vel[c], 0.0)[0]
            den_ref[tx, ty, tz, :] = jnp.where(live, new_rho, 0.0)[0]
        else:
            updated = jnp.concatenate(new_off + new_vel + [new_rho, tile[7:8]], axis=0)
            outs[0][place] = jnp.where(live, updated, tile)


def pair_sums(own, src, part, targets, columns, layers_of, final, chain=8, skip=()):
    nx, ny, nz = targets
    slots = src.shape[-1]
    ranges = []
    for tx in range(nx):
        near = [k for k, x in enumerate(columns) if abs(x - tx) <= 1 and (tx, x) not in skip]
        near = near or [0, -1]
        assert near == list(range(near[0], near[-1] + 1)) or near == [0, -1]
        ranges.append((near[0], near[-1] + 1))
    if final == "last":
        out_shape = (
            jax.ShapeDtypeStruct((3, nx, ny, nz, slots), jnp.float32),
            jax.ShapeDtypeStruct((3, nx, ny, nz, slots), jnp.float32),
            jax.ShapeDtypeStruct((nx, ny, nz, slots), jnp.float32),
        )
    else:
        out_shape = jax.ShapeDtypeStruct((nx, ny, nz, ROWS, slots), jnp.float32)
    kernel = functools.partial(
        pair_kernel,
        targets=targets,
        columns=columns,
        ranges=ranges,
        slots=slots,
        layers_of=layers_of,
        has_part=part is not None,
        final=final,
        chain=chain,
    )
    args = (own, src) if part is None else (own, src, part)
    vmem = pl.BlockSpec(memory_space=pltpu.VMEM)
    count = nx * ny * nz
    trips = -(-9 // UNROLL) * len(columns) * ny * nz
    tiles = (trips + 2) * UNROLL
    items = -(-9 // UNROLL) * 3 * count + 2 * chain + 1 + 3 * -(-9 // UNROLL)
    wide = UNROLL * FORMS * slots
    return pl.pallas_call(
        kernel,
        out_shape=out_shape,
        in_specs=[vmem] * len(args),
        out_specs=jax.tree.map(lambda _: vmem, out_shape),
        scratch_shapes=[
            pltpu.VMEM((tiles, ROWS, slots), jnp.float32),
            pltpu.VMEM((tiles, 3, 16, FORMS * slots), jnp.bfloat16),
            pltpu.VMEM((tiles, 32, slots), jnp.bfloat16),
            pltpu.VMEM((count, slots, slots), jnp.bfloat16),
            pltpu.VMEM((count, slots, slots), jnp.float32),
            pltpu.VMEM((count, slots, slots), jnp.float32),
            pltpu.VMEM((slots, wide), jnp.float32),
            pltpu.VMEM((slots, wide), jnp.float32),
            pltpu.VMEM((count, slots, slots), jnp.float32),
            pltpu.SMEM((src.shape[0] * src.shape[1] * src.shape[2] + count,), jnp.int32),
            pltpu.SMEM((2, items), jnp.int32),
        ],
        compiler_params=pltpu.CompilerParams(vmem_limit_bytes=24 << 20),
        cost_estimate=pl.CostEstimate(
            flops=count * 9 * len(columns) * slots * slots * 40, bytes_accessed=src.size * 4, transcendentals=0
        ),
    )(*args)


def per_device(offsets, velocity, density, counts):
    wide, tall, deep = offsets.shape[1:4]
    tile = pack(offsets, velocity, density, counts)

    def ends(block, dim):
        size = block.shape[dim]
        first = lax.slice_in_dim(block, 0, 1, axis=dim)
        return first, lax.slice_in_dim(block, size - 1, size, axis=dim)

    def with_layers(block):
        first, last = ends(block, 2)
        if lax.axis_size("gz") == 1:
            return block, lambda z: z % deep
        if lax.axis_size("gz") * deep == 2:
            return jnp.concatenate([block, from_after(first, "gz")], axis=2), lambda z: z % 2
        size = lax.axis_size("gz")
        parts = [block, from_after(first, "gz"), from_after(last, "gz", size - 1)]
        return jnp.concatenate(parts, axis=2), lambda z: z % (deep + 2)

    def with_rows(block):
        before, after = neighbours(*ends(block, 1), "gy")
        return jnp.concatenate([before, block, after], axis=1)

    targets = (wide, tall, deep)
    assert wide >= 2

    block, layer = with_layers(tile)
    own = with_rows(block)
    layers_of = lambda z: (layer(z - 1), layer(z), layer(z + 1))
    before, after = neighbours(*ends(own, 0), "gx")
    inside = pair_sums(own, own, None, targets, tuple(range(wide)), layers_of, None)
    outside = jnp.concatenate([before, after], axis=0)
    state = pair_sums(own, outside, inside, targets, (-1, wide), layers_of, "step")

    block, layer = with_layers(state)
    own = with_rows(block)
    next_two = from_after(own[0:2], "gx")
    here = tuple(range(-1, wide - 1))
    inside = pair_sums(
        own[1:], own, None, (wide - 1, tall, deep), here, layers_of, None
    )
    done = {(tx, x) for tx in range(wide - 1) for x in here}
    src = jnp.concatenate([own[1:], next_two], axis=0)
    columns = tuple(range(0, wide + 1))
    return pair_sums(src[:wide], src, inside, targets, columns, layers_of, "last", skip=done)


def solution(mesh):
    return jax.shard_map(
        per_device,
        mesh=mesh,
        in_specs=(
            P(None, "gx", "gy", "gz", None),
            P(None, "gx", "gy", "gz", None),
            P("gx", "gy", "gz", None),
            P("gx", "gy", "gz"),
        ),
        out_specs=(
            P(None, "gx", "gy", "gz", None),
            P(None, "gx", "gy", "gz", None),
            P("gx", "gy", "gz", None),
        ),
        check_vma=False,
    )
```
